32 devices in a mesh: dp: 8 (over y, x, core), tensor: 4 (over z).
Axes of the slice: x: 2, y: 2, z: 4, core: 2. Of those that a mesh axis runs over, the one named last changes fastest.
Arguments:
- tokens: bfloat16 [8192, 768], P('dp'), may hold values from -6 to 6
- lengths: int32 [16], P('dp'), may hold values from 64 to 512
- dropped: int32 [16], P('dp'), may hold values 0 or 1
- queryproj: bfloat16 [768, 768], P(None, 'tensor'), may hold values from -0.21875 to 0.21875
- querybias: float32 [768], P('tensor'), may hold values from -2 to 2
- keyproj: bfloat16 [768, 768], P(None, 'tensor'), may hold values from -0.21875 to 0.21875
- valueproj: bfloat16 [768, 768], P(None, 'tensor'), may hold values from -0.21875 to 0.21875
- valuebias: float32 [768], P('tensor'), may hold values from -2 to 2
- outproj: bfloat16 [768, 768], P('tensor'), may hold values from -0.875 to 0.875
- outbias: float32 [768], replicated, may hold values from -2 to 2
- gainone: float32 [768], replicated, may hold values from 0.25 to 1.75
- shiftone: float32 [768], replicated, may hold values from -2 to 2
- upproj: bfloat16 [768, 3072], P(None, 'tensor'), may hold values from -0.21875 to 0.21875
- upbias: float32 [3072], P('tensor'), may hold values from -2 to 2
- downproj: bfloat16 [3072, 768], P('tensor'), may hold values from -0.109375 to 0.109375
- downbias: float32 [768], replicated, may hold values from -2 to 2
- gaintwo: float32 [768], replicated, may hold values from 0.25 to 1.75
- shifttwo: float32 [768], replicated, may hold values from -2 to 2
- cotangent: bfloat16 [8192, 768], P(('dp', 'tensor')), may hold values from -6 to 6
Outputs:
- outputs: bfloat16 [8192, 768], P(('dp', 'tensor'))
- input_grad: float32 [8192, 768], P(('dp', 'tensor'))
- queryproj_grad: float32 [768, 768], P(None, 'tensor')
- querybias_grad: float32 [768], P('tensor')
- keyproj_grad: float32 [768, 768], P(None, 'tensor')
- valueproj_grad: float32 [768, 768], P(None, 'tensor')
- valuebias_grad: float32 [768], P('tensor')
- outproj_grad: float32 [768, 768], P('tensor')
- outbias_grad: float32 [768], replicated
- gainone_grad: float32 [768], replicated
- shiftone_grad: float32 [768], replicated
- upproj_grad: float32 [768, 3072], P(None, 'tensor')
- upbias_grad: float32 [3072], P('tensor')
- downproj_grad: float32 [3072, 768], P('tensor')
- downbias_grad: float32 [768], replicated
- gaintwo_grad: float32 [768], replicated
- shifttwo_grad: float32 [768], replicated
The draws below stay inside these ranges and needn't reach their ends.
Inputs may be any that keep to these rules, and one draw needn't show every extreme that they name: `lengths`: rows of a sequence at or beyond its length are padding. `dropped`: a flag of 1 makes the layer the identity for that sequence.
All inputs are finite; a program needn't handle non-finite values. No bound on the sum of `dropped` on one device may be relied on, other than what follows from the above.
Results may differ from the reference program's by a relative error of at most 0.014.
Values may be sent and summed in bfloat16 or wider, within the bound.
No kernel may reach another device: no remote copies, remote signals or barrier semaphores. Data moves between devices by JAX's collectives and lax.ppermute only.
A program may use at most 128 MiB of HBM per device.

```python
import jax
import jax.numpy as jnp
from jax import lax

D = 768
H = 12
HD = 64
FF = 3072
L = 512
SEQS = 16
TOKENS = 8192


def plant(values, rng, least, largest):
    extent = values.shape
    index_at = [jax.random.randint(jax.random.fold_in(rng, axis), (), 0, extent[axis]) for axis in range(len(extent))]
    values = values.at[tuple(index_at)].set(least)
    longest = extent.index(max(extent))
    index_at[longest] = (index_at[longest] + 1) % extent[longest]
    return values.at[tuple(index_at)].set(largest)


def shard_levels(rng, extent, split, low, top_value):
    factor_of, own = 1.0, jax.random.fold_in(rng, 6)
    for axis_at, shards_of in split:
        draws = jnp.exp(jax.random.uniform(jax.random.fold_in(own, axis_at), (shards_of,), jnp.float32, low / len(split), top_value / len(split)))
        factor_of = factor_of * jnp.repeat(draws, extent[axis_at] // shards_of).reshape([-1 if axis == axis_at else 1 for axis in range(len(extent))])
    return factor_of


def noise(rng, extent, scale, reach, split=(), dtype=jnp.bfloat16):
    values = jax.random.normal(rng, extent, jnp.float32) * scale
    if len(split) > 0:
        values = shard_levels(rng, extent, split, -0.22, 0.18) * values
    return jnp.clip(values, min=-reach, max=reach).astype(dtype)


def setup_inputs(seed: int = 0) -> dict:
    splits = jax.random.split(jax.random.key(seed), 20)
    tokens = noise(splits[0], (TOKENS, D), 1.0, 6.0, ((0, 8),))
    lengths = plant(jax.random.randint(splits[1], (SEQS,), L // 8, L + 1), jax.random.fold_in(splits[1], 1), L // 8, L).astype(jnp.int32)
    dropped = plant((jax.random.randint(splits[2], (SEQS,), 0, 5) < 1).astype(jnp.int32), jax.random.fold_in(splits[2], 1), 0, 1)
    queryproj = noise(splits[3], (D, H * HD), D ** -0.5, 0.21875, ((1, 4),))
    querybias = noise(splits[4], (H * HD,), 0.3, 2.0, ((0, 4),), jnp.float32)
    keyproj = noise(splits[5], (D, H * HD), D ** -0.5, 0.21875, ((1, 4),))
    valueproj = noise(splits[6], (D, H * HD), D ** -0.5, 0.21875, ((1, 4),))
    valuebias = noise(splits[7], (H * HD,), 0.3, 2.0, ((0, 4),), jnp.float32)
    outproj = noise(splits[8], (H * HD, D), (D // 16) ** -0.5, 0.875, ((0, 4),))
    outbias = noise(splits[9], (D,), 0.3, 2.0, (), jnp.float32)
    gainone = jnp.clip(1.0 + 0.15 * jax.random.normal(splits[10], (D,), jnp.float32), 0.25, 1.75)
    shiftone = noise(splits[11], (D,), 0.3, 2.0, (), jnp.float32)
    upproj = noise(splits[12], (D, FF), D ** -0.5, 0.21875, ((1, 4),))
    upbias = noise(splits[13], (FF,), 0.3, 2.0, ((0, 4),), jnp.float32)
    downproj = noise(splits[14], (FF, D), FF ** -0.5, 0.109375, ((0, 4),))
    downbias = noise(splits[15], (D,), 0.3, 2.0, (), jnp.float32)
    gaintwo = jnp.clip(1.0 + 0.15 * jax.random.normal(splits[16], (D,), jnp.float32), 0.25, 1.75)
    shifttwo = noise(splits[17], (D,), 0.3, 2.0, (), jnp.float32)
    cotangent = noise(splits[18], (TOKENS, D), 1.0, 6.0, ((0, 32),))
    return dict(tokens=tokens, lengths=lengths, dropped=dropped, queryproj=queryproj, querybias=querybias, keyproj=keyproj, valueproj=valueproj, valuebias=valuebias, outproj=outproj, outbias=outbias, gainone=gainone, shiftone=shiftone, upproj=upproj, upbias=upbias, downproj=downproj, downbias=downbias, gaintwo=gaintwo, shifttwo=shifttwo, cotangent=cotangent)


EPS = 1e-05

@jax.custom_vjp
def low(v):
    return lax.optimization_barrier(v.astype(jnp.bfloat16)).astype(jnp.float32)

@jax.custom_vjp
def low_back(v):
    return v

def low_keep(v):
    return (low(v), None)

def low_pass(kept, grad):
    return (grad,)

def back_keep(v):
    return (v, None)

def back_low(kept, grad):
    return (low(grad),)
low.defvjp(low_keep, low_pass)
low_back.defvjp(back_keep, back_low)

def matmul(left, right):
    return jnp.dot(left, right, precision=lax.Precision.HIGHEST, preferred_element_type=jnp.float32)

def gelu_exact(inner):
    return 0.5 * inner * (1.0 + jax.scipy.special.erf(inner * 0.7071067811865476))

def layer_norm(value, gain, shift):
    center = lax.optimization_barrier(jnp.mean(value, axis=-1, keepdims=True))
    centered = value - center
    variance = lax.optimization_barrier(jnp.mean(centered * centered, axis=-1, keepdims=True))
    return centered * lax.rsqrt(variance + EPS) * gain + shift

def sequence_forward(source, length, flag, queryproj, querybias, keyproj, valueproj, valuebias, outproj, outbias, gainone, shiftone, upproj, upbias, downproj, downbias, gaintwo, shifttwo):
    low_source = low(source)
    queries = low(low_back(matmul(low_source, queryproj) + querybias)).reshape(L, H, HD)
    keys_mat = low(low_back(matmul(low_source, keyproj))).reshape(L, H, HD)
    values_mat = low(low_back(matmul(low_source, valueproj) + valuebias)).reshape(L, H, HD)
    scores = jnp.einsum('qhd,khd->hqk', queries, keys_mat, precision=lax.Precision.HIGHEST) * HD ** (-0.5)
    scores = low_back(scores)
    key_ok = jnp.arange(L) < length
    scores = jnp.where(key_ok[None, None, :], scores, -1000000000.0)
    row_max = lax.optimization_barrier(jnp.max(scores, axis=-1, keepdims=True))
    expon = jnp.exp(scores - row_max)
    attn_prob = expon / lax.optimization_barrier(jnp.sum(expon, axis=-1, keepdims=True))
    context = jnp.einsum('hqk,khd->qhd', low(attn_prob), values_mat, precision=lax.Precision.HIGHEST)
    context = low(low_back(context.reshape(L, H * HD)))
    attended = source + low_back(matmul(context, outproj)) + outbias
    normed = layer_norm(attended, gainone, shiftone)
    inner_sum = low_back(matmul(low(normed), upproj) + upbias)
    activated = low(gelu_exact(inner_sum))
    mixed = normed + low_back(matmul(activated, downproj)) + downbias
    layer_out = layer_norm(mixed, gaintwo, shifttwo)
    keep_flag = (1 - flag).astype(jnp.float32)
    return keep_flag * layer_out + (1.0 - keep_flag) * source

def reference(tokens, lengths, dropped, queryproj, querybias, keyproj, valueproj, valuebias, outproj, outbias, gainone, shiftone, upproj, upbias, downproj, downbias, gaintwo, shifttwo, cotangent):
    params = tuple((weight.astype(jnp.float32) for weight in (queryproj, querybias, keyproj, valueproj, valuebias, outproj, outbias, gainone, shiftone, upproj, upbias, downproj, downbias, gaintwo, shifttwo)))
    seq_count = tokens.shape[0] // L
    sources = tokens.astype(jnp.float32).reshape(seq_count, L, D)
    cotangents = cotangent.astype(jnp.float32).reshape(seq_count, L, D)

    def per_sequence(accum, operands):
        source, cot_rows, length, flag = operands

        def forward(source_in, *weights):
            return sequence_forward(source_in, length, flag, *weights)
        result, pullback = jax.vjp(forward, source, *params)
        valid_rows = (jnp.arange(L) < length).astype(jnp.float32)[:, None]
        grads = pullback(cot_rows * valid_rows)
        summed = tuple((before + added for before, added in zip(accum, grads[1:])))
        return (summed, (result.astype(jnp.bfloat16), grads[0]))
    zeros = tuple((jnp.zeros_like(weight) for weight in params))
    totals, (outputs, input_grad) = lax.scan(per_sequence, zeros, (sources, cotangents, lengths, dropped))
    return (outputs.reshape(seq_count * L, D), input_grad.reshape(seq_count * L, D), totals[0], totals[1], totals[2], totals[3], totals[4], totals[5], totals[6], totals[7], totals[8], totals[9], totals[10], totals[11], totals[12], totals[13], totals[14])
```

```python
import jax
import jax.numpy as jnp
from jax import lax
from jax.sharding import PartitionSpec as P

HD = 64
L = 512
EPS = 1e-05
GROUP = 8
BF = jnp.bfloat16
F32 = jnp.float32


def nn(left, right):
    return jnp.dot(left, right, preferred_element_type=F32)


def nt(left, right):
    return lax.dot_general(left, right, (((1,), (1,)), ((), ())), preferred_element_type=F32)


def tn(left, right):
    return lax.dot_general(left, right, (((0,), (0,)), ((), ())), preferred_element_type=F32)


def gelu_parts(inner):
    cumul = 0.5 * (1.0 + jax.scipy.special.erf(inner * 0.7071067811865476))
    slope = cumul + inner * jnp.exp(-0.5 * inner * inner) * 0.3989422804014327
    return inner * cumul, slope


def norm_forward(value, gain, shift):
    center = jnp.mean(value, axis=-1, keepdims=True)
    centered = value - center
    rscale = lax.rsqrt(jnp.mean(centered * centered, axis=-1, keepdims=True) + EPS)
    normal = centered * rscale
    return normal * gain + shift, normal, rscale


def norm_backward(grad_rows, normal, rscale, gain):
    scaled = grad_rows * gain
    return rscale * (
        scaled
        - jnp.mean(scaled, axis=-1, keepdims=True)
        - normal * jnp.mean(scaled * normal, axis=-1, keepdims=True)
    )


def heads_of(array):
    return array.reshape(array.shape[0], -1, HD)


def scores_of(q, k, key_ok):
    scores = jnp.einsum("qhd,khd->hqk", heads_of(q), heads_of(k), preferred_element_type=F32)
    return jnp.where(key_ok[None, None, :], scores * HD ** (-0.5), -1000000000.0)


def attn_forward(x, pack, qb, vb, key_ok):
    w = pack.shape[1] // 4
    qkv = nn(x, pack[:, : 3 * w])
    q = (qkv[:, :w] + qb).astype(BF)
    k = qkv[:, w : 2 * w].astype(BF)
    v = (qkv[:, 2 * w :] + vb).astype(BF)
    scores = scores_of(q, k, key_ok)
    row_max = jnp.max(scores, axis=-1, keepdims=True)
    expon = jnp.exp(scores - row_max)
    row_sum = jnp.sum(expon, axis=-1, keepdims=True)
    prob = (expon / row_sum).astype(BF)
    ctx = jnp.einsum("hqk,khd->qhd", prob, heads_of(v), preferred_element_type=F32)
    ctx = ctx.astype(BF).reshape(x.shape[0], w)
    return (q, k, v, ctx, row_max + jnp.log(row_sum)), nt(ctx, pack[:, 3 * w :])


def attn_backward(x, d_proj, pack, saved, key_ok):
    q, k, v, ctx, lse = saved
    w = pack.shape[1] // 4
    rows = x.shape[0]
    d_ctx = nn(d_proj, pack[:, 3 * w :]).astype(BF)
    prob = jnp.exp(scores_of(q, k, key_ok) - lse)
    d_prob = jnp.einsum("qhd,khd->hqk", heads_of(d_ctx), heads_of(v), preferred_element_type=F32)
    centre = jnp.sum(prob * d_prob, axis=-1, keepdims=True)
    d_scores = (prob * (d_prob - centre)).astype(BF)
    scale = HD ** (-0.5)
    d_q = jnp.einsum("hqk,khd->qhd", d_scores, heads_of(k), preferred_element_type=F32) * scale
    d_k = jnp.einsum("hqk,qhd->khd", d_scores, heads_of(q), preferred_element_type=F32) * scale
    d_v = jnp.einsum("hqk,qhd->khd", prob.astype(BF), heads_of(d_ctx), preferred_element_type=F32)
    d_qkv = jnp.concatenate(
        [d.astype(BF).reshape(rows, w) for d in (d_q, d_k, d_v)], axis=1
    )
    grad = jnp.concatenate([tn(x, d_qkv), tn(d_proj, ctx)], axis=1).astype(BF)
    sums = jnp.sum(d_qkv, axis=0, dtype=F32)
    return grad, sums[:w], sums[2 * w :], nt(d_qkv, pack[:, : 3 * w])


def slot(rel):
    return (rel >> 1) | ((rel & 1) << 2)


def make_per_device(dp_count, tensor_count):
    def zx(array, step):
        return lax.ppermute(array, "tensor", [(i, i ^ step) for i in range(tensor_count)])

    def dx(array, step):
        return lax.ppermute(array, "dp", [(i, i ^ step) for i in range(dp_count)])

    def gather_group(piece):
        four = jnp.concatenate([piece] + [dx(piece, step) for step in (2, 4, 6)], axis=0)
        return four, dx(four, 1)

    def in_order(halves, me, count):
        whole = jnp.concatenate(halves, axis=0)
        chunk = whole.shape[0] // GROUP
        whole = whole.reshape(GROUP, chunk, whole.shape[1])
        parts = [lax.dynamic_index_in_dim(whole, slot(j ^ me), 0, False) for j in range(GROUP)]
        rows = chunk // count
        return [
            jnp.concatenate([part[i * rows : (i + 1) * rows] for part in parts], axis=0)
            for i in range(count)
        ]

    def relative(grads, me):
        rows = grads[0].shape[0] // GROUP
        chunks = []
        for rel in (0, 2, 4, 6, 1, 3, 5, 7):
            for grad in grads:
                chunks.append(lax.dynamic_slice_in_dim(grad, (me ^ rel) * rows, rows, 0))
        return jnp.concatenate(chunks, axis=0)

    def scatter_group(stacked):
        half = stacked.shape[0] // 2
        total = stacked[:half].astype(F32) + dx(stacked[half:], 1).astype(F32)
        quarter = half // 4
        out = total[:quarter]
        low = total[quarter:].astype(BF)
        for i, step in enumerate((2, 4, 6)):
            out = out + dx(low[i * quarter : (i + 1) * quarter], step).astype(F32)
        step = GROUP
        while step < dp_count:
            out = out + dx(out.astype(BF), step).astype(F32)
            step *= 2
        return out

    def per_device(
        tokens, lengths, dropped, queryproj, querybias, keyproj, valueproj, valuebias,
        outproj, outbias, gainone, shiftone, upproj, upbias, downproj, downbias,
        gaintwo, shifttwo, cotangent,
    ):
        share = cotangent.shape[0]
        width = tokens.shape[1]
        heads_width = queryproj.shape[1]
        z = lax.axis_index("tensor")
        me = lax.axis_index("dp") & (GROUP - 1)
        seq, half = z >> 1, z & 1
        length = lax.dynamic_index_in_dim(lengths, seq, 0, False)
        keep = 1.0 - lax.dynamic_index_in_dim(dropped, seq, 0, False).astype(F32)

        chunk = width // GROUP
        first = me * chunk
        piece_attn = jnp.concatenate(
            [lax.dynamic_slice_in_dim(a, first, chunk, 0) for a in (queryproj, keyproj, valueproj)]
            + [lax.dynamic_slice_in_dim(outproj, first, chunk, 1).T],
            axis=1,
        )
        piece_ffn = jnp.concatenate(
            [lax.dynamic_slice_in_dim(a, first, chunk, 0) for a in (upproj, downproj)], axis=0
        )
        biases = jnp.concatenate([querybias, valuebias, upbias]).reshape(1, -1)
        piece_attn = zx(piece_attn, 2)
        biases_far = zx(biases, 2)
        cot_far = zx(cotangent, 1)
        attn_halves = gather_group(piece_attn)
        piece_ffn = zx(piece_ffn, 2)
        ffn_halves = gather_group(piece_ffn)

        x_own = lax.dynamic_slice_in_dim(tokens, z * share, share, 0)
        x_far = lax.dynamic_slice_in_dim(tokens, (z ^ 1) * share, share, 0)
        x = jnp.concatenate([x_own, x_far], axis=0)
        base = jnp.arange(share, dtype=jnp.int32)
        position = jnp.concatenate([base + half * share, base + (1 - half) * share])
        valid = position < length
        bias_of = []
        for row in (biases[0], biases_far[0]):
            bias_of.append((row[:heads_width], row[heads_width : 2 * heads_width], row[2 * heads_width :]))

        pack_near = jnp.concatenate([queryproj, keyproj, valueproj, outproj.T], axis=1)
        packs = [pack_near]
        saved, partial = [], 0.0
        for block in range(2):
            if block == 1:
                packs.append(in_order(attn_halves, me, 1)[0])
            keep_block, part = attn_forward(x, packs[block], *bias_of[block][:2], valid)
            saved.append(keep_block)
            partial = partial + part

        def pair_sum(own_part):
            low = own_part.astype(BF)
            return own_part + jnp.concatenate(
                [zx(low[share:], 1), zx(low[:share], 1)], axis=0
            ).astype(F32)

        source = x.astype(F32)
        attended = source + pair_sum(partial) + outbias
        normed, normal_one, rscale_one = norm_forward(attended, gainone, shiftone)
        normed_low = normed.astype(BF)
        ups, downs = [upproj], [downproj]
        far_up, far_down = in_order(ffn_halves, me, 2)
        ups.append(far_up)
        downs.append(far_down)
        acts, slopes, branch = [], [], 0.0
        for block in range(2):
            act, slope = gelu_parts(nn(normed_low, ups[block]) + bias_of[block][2])
            acts.append(act.astype(BF))
            slopes.append(slope)
            branch = branch + nn(acts[block], downs[block])
        mixed = normed + pair_sum(branch) + downbias
        layer, normal_two, rscale_two = norm_forward(mixed, gaintwo, shifttwo)
        outputs = (keep * layer + (1.0 - keep) * source)[:share].astype(BF)

        cot = jnp.concatenate([cotangent, cot_far], axis=0).astype(F32)
        d_out = cot * valid.astype(F32)[:, None]
        d_layer = keep * d_out
        d_mixed = norm_backward(d_layer, normal_two, rscale_two, gaintwo)
        d_branch = d_mixed.astype(BF)
        up_sums, ffn_slices, part = [], [], 0.0
        for block in range(2):
            d_inner = (nt(d_branch, downs[block]) * slopes[block]).astype(BF)
            up_sums.append(jnp.sum(d_inner, axis=0, dtype=F32))
            down_grad = tn(acts[block], d_branch).astype(BF)
            up_grad = tn(normed_low, d_inner).astype(BF)
            part = part + nt(d_inner, ups[block])
            ffn_slices.append(scatter_group(relative([up_grad, down_grad], me)))
        d_normed = d_mixed + pair_sum(part)
        d_attended = norm_backward(d_normed, normal_one, rscale_one, gainone)
        d_proj = d_attended.astype(BF)
        ffn_slice = ffn_slices[0] + zx(ffn_slices[1].astype(BF), 2).astype(F32)
        ffn_grads = in_order(gather_group(ffn_slice.astype(BF)), me, 2)

        attn_slices, attn_sums, part = [], [], 0.0
        for block in (1, 0):
            grad, q_sum, v_sum, back = attn_backward(x, d_proj, packs[block], saved[block], valid)
            attn_slices.append(scatter_group(relative([grad], me)))
            attn_sums.append((q_sum, v_sum))
            part = part + back
        attn_slices.reverse()
        attn_sums.reverse()
        input_grad = (
            part[:share] + zx(part[share:].astype(BF), 1).astype(F32)
            + d_attended[:share] + (1.0 - keep) * d_out[:share]
        )
        attn_slice = attn_slices[0] + zx(attn_slices[1].astype(BF), 2).astype(F32)
        (attn_grad,) = in_order(gather_group(attn_slice.astype(BF)), me, 1)
        attn_grad = attn_grad.astype(F32)

        own = slice(0, share)
        rows = [
            jnp.sum(d_attended[own], axis=0),
            jnp.sum(d_normed[own] * normal_one[own], axis=0),
            jnp.sum(d_normed[own], axis=0),
            jnp.sum(d_mixed[own], axis=0),
            jnp.sum(d_layer[own] * normal_two[own], axis=0),
            jnp.sum(d_layer[own], axis=0),
        ]
        pad = jnp.zeros((width - 2 * heads_width,), F32)
        near = jnp.stack(rows + [jnp.concatenate(attn_sums[0] + (pad,)), up_sums[0]])
        far = jnp.stack([jnp.concatenate(attn_sums[1] + (pad,)), up_sums[1]])
        small = jnp.concatenate([near, far], axis=0)
        step = 1
        while step < dp_count:
            small = small + dx(small, step)
            step *= 2
        vectors = small[:6]
        vectors = vectors + zx(vectors, 1)
        other = zx(jnp.concatenate([vectors, small[8:10]], axis=0), 2)
        vectors = vectors + other[:6]
        sums = small[6:8] + other[6:8]
        w = heads_width
        return (
            outputs,
            input_grad,
            attn_grad[:, :w],
            sums[0, :w],
            attn_grad[:, w : 2 * w],
            attn_grad[:, 2 * w : 3 * w],
            sums[0, w : 2 * w],
            attn_grad[:, 3 * w :].T,
            vectors[0],
            vectors[1],
            vectors[2],
            ffn_grads[0].astype(F32),
            sums[1],
            ffn_grads[1].astype(F32),
            vectors[3],
            vectors[4],
            vectors[5],
        )

    return per_device


def solution(mesh):
    both = P(("dp", "tensor"), None)
    column, row, unit = P(None, "tensor"), P("tensor", None), P("tensor")
    return jax.shard_map(
        make_per_device(mesh.shape["dp"], mesh.shape["tensor"]),
        mesh=mesh,
        in_specs=(
            P("dp", None), P("dp"), P("dp"), column, unit, column, column, unit, row,
            P(), P(), P(), column, unit, row, P(), P(), P(), both,
        ),
        out_specs=(
            both, both, column, unit, column, column, unit, row, P(), P(), P(),
            column, unit, row, P(), P(), P(),
        ),
        check_vma=False,
    )
```

```python
import jax
import jax.numpy as jnp
from jax import lax
from jax.experimental import pallas as pl
from jax.experimental.pallas import tpu as pltpu
from jax.sharding import PartitionSpec as P

HD = 64
L = 512
EPS = 1e-05
GROUP = 8
BF = jnp.bfloat16
F32 = jnp.float32


def nn(left, right):
    return jnp.dot(left, right, preferred_element_type=F32)


def nt(left, right):
    return lax.dot_general(left, right, (((1,), (1,)), ((), ())), preferred_element_type=F32)


def tn(left, right):
    return lax.dot_general(left, right, (((0,), (0,)), ((), ())), preferred_element_type=F32)


def gelu_parts(inner):
    cumul = 0.5 * (1.0 + jax.scipy.special.erf(inner * 0.7071067811865476))
    slope = cumul + inner * jnp.exp(-0.5 * inner * inner) * 0.3989422804014327
    return inner * cumul, slope


def norm_forward(value, gain, shift):
    center = jnp.mean(value, axis=-1, keepdims=True)
    centered = value - center
    rscale = lax.rsqrt(jnp.mean(centered * centered, axis=-1, keepdims=True) + EPS)
    normal = centered * rscale
    return normal * gain + shift, normal, rscale


def norm_backward(grad_rows, normal, rscale, gain):
    scaled = grad_rows * gain
    return rscale * (
        scaled
        - jnp.mean(scaled, axis=-1, keepdims=True)
        - normal * jnp.mean(scaled * normal, axis=-1, keepdims=True)
    )


def heads_of(array):
    return array.reshape(array.shape[0], -1, HD)


def scores_of(q, k, key_ok):
    scores = jnp.einsum("qhd,khd->hqk", heads_of(q), heads_of(k), preferred_element_type=F32)
    return jnp.where(key_ok[None, None, :], scores * HD ** (-0.5), -1000000000.0)


def attn_forward(x, pack, qb, vb, key_ok):
    w = pack.shape[1] // 4
    qkv = nn(x, pack[:, : 3 * w])
    q = (qkv[:, :w] + qb).astype(BF)
    k = qkv[:, w : 2 * w].astype(BF)
    v = (qkv[:, 2 * w :] + vb).astype(BF)
    scores = scores_of(q, k, key_ok)
    row_max = jnp.max(scores, axis=-1, keepdims=True)
    expon = jnp.exp(scores - row_max)
    row_sum = jnp.sum(expon, axis=-1, keepdims=True)
    prob = (expon / row_sum).astype(BF)
    ctx = jnp.einsum("hqk,khd->qhd", prob, heads_of(v), preferred_element_type=F32)
    ctx = ctx.astype(BF).reshape(x.shape[0], w)
    return (q, k, v, ctx, row_max + jnp.log(row_sum)), nt(ctx, pack[:, 3 * w :])


def attn_backward(x, d_proj, pack, saved, key_ok, me):
    q, k, v, ctx, lse = saved
    w = pack.shape[1] // 4
    rows = x.shape[0]
    d_ctx = nn(d_proj, pack[:, 3 * w :]).astype(BF)
    prob = jnp.exp(scores_of(q, k, key_ok) - lse)
    d_prob = jnp.einsum("qhd,khd->hqk", heads_of(d_ctx), heads_of(v), preferred_element_type=F32)
    centre = jnp.sum(prob * d_prob, axis=-1, keepdims=True)
    d_scores = (prob * (d_prob - centre)).astype(BF)
    scale = HD ** (-0.5)
    d_q = jnp.einsum("hqk,khd->qhd", d_scores, heads_of(k), preferred_element_type=F32) * scale
    d_k = jnp.einsum("hqk,qhd->khd", d_scores, heads_of(q), preferred_element_type=F32) * scale
    d_v = jnp.einsum("hqk,qhd->khd", prob.astype(BF), heads_of(d_ctx), preferred_element_type=F32)
    d_qkv = jnp.concatenate(
        [d.astype(BF).reshape(rows, w) for d in (d_q, d_k, d_v)], axis=1
    )
    grad = attn_weight_grads(x, d_qkv, d_proj, ctx, me)
    sums = jnp.sum(d_qkv, axis=0, dtype=F32)
    return grad, sums[:w], sums[2 * w :], nt(d_qkv, pack[:, : 3 * w])


RELATIVE = (0, 2, 4, 6, 1, 3, 5, 7)
SMEM = pl.BlockSpec(memory_space=pltpu.SMEM)
VMEM = pl.BlockSpec(memory_space=pltpu.VMEM)


def shape_of(shape, dtype):
    return jax.ShapeDtypeStruct(shape, dtype)


def chunk_at(me, rel, rows):
    return pl.ds(pl.multiple_of((me ^ rel) * rows, 32), rows)


def halves_chunks(four, other, rows):
    for i, rel in enumerate(RELATIVE):
        source = four if i < GROUP // 2 else other
        yield rel, source, (i % (GROUP // 2)) * rows


def in_order(halves, me, count, dtype):
    rows = halves[0].shape[0] // (GROUP // 2)
    part, width = rows // count, halves[0].shape[1]

    def kernel(me_ref, four, other, *outs):
        mine = me_ref[0]
        for rel, source, start in halves_chunks(four, other, rows):
            for i, out in enumerate(outs):
                chunk = source[start + i * part : start + (i + 1) * part, :]
                out[chunk_at(mine, rel, part), :] = chunk.astype(dtype)

    return pl.pallas_call(
        kernel,
        out_shape=[shape_of((GROUP * part, width), dtype)] * count,
        in_specs=[SMEM, VMEM, VMEM],
        out_specs=[VMEM] * count,
        name="in_order",
    )(me, *halves)


def attn_outputs(halves, me, w):
    rows = halves[0].shape[0] // (GROUP // 2)
    width = halves[0].shape[1]

    def kernel(me_ref, four, other, q, k, v, o, scratch):
        mine = me_ref[0]
        for rel, source, start in halves_chunks(four, other, rows):
            scratch[chunk_at(mine, rel, rows), :] = source[start : start + rows, :].astype(F32)
        q[...] = scratch[:, :w]
        k[...] = scratch[:, w : 2 * w]
        v[...] = scratch[:, 2 * w : 3 * w]
        o[...] = scratch[:, 3 * w :].T

    tall, wide = shape_of((GROUP * rows, w), F32), shape_of((w, GROUP * rows), F32)
    return pl.pallas_call(
        kernel,
        out_shape=[tall, tall, tall, wide],
        in_specs=[SMEM, VMEM, VMEM],
        out_specs=[VMEM] * 4,
        scratch_shapes=[pltpu.VMEM((GROUP * rows, width), F32)],
        name="attn_outputs",
    )(me, *halves)


def weight_grads(pairs, me):
    total, width = pairs[0][0].shape[1], pairs[0][1].shape[1]
    rows, count = total // GROUP, len(pairs)

    def kernel(me_ref, *refs):
        mine = me_ref[0]
        out, scratch = refs[-2:]
        for i in range(count):
            scratch[...] = tn(refs[2 * i][...], refs[2 * i + 1][...])
            for j, rel in enumerate(RELATIVE):
                start = (j * count + i) * rows
                out[start : start + rows, :] = scratch[chunk_at(mine, rel, rows), :].astype(BF)

    return pl.pallas_call(
        kernel,
        out_shape=shape_of((total * count, width), BF),
        in_specs=[SMEM] + [VMEM] * (2 * count),
        out_specs=VMEM,
        scratch_shapes=[pltpu.VMEM((total, width), F32)],
        name="weight_grads",
    )(me, *[array for pair in pairs for array in pair])


def attn_weight_grads(x, d_qkv, d_proj, ctx, me):
    total = x.shape[1]
    rows = total // GROUP
    w = ctx.shape[1]

    def kernel(me_ref, x_ref, d_ref, p_ref, c_ref, out, scratch):
        mine = me_ref[0]
        scratch[:, : 3 * w] = tn(x_ref[...], d_ref[...])
        scratch[:, 3 * w :] = tn(p_ref[...], c_ref[...])
        for j, rel in enumerate(RELATIVE):
            out[j * rows : (j + 1) * rows, :] = scratch[chunk_at(mine, rel, rows), :].astype(BF)

    return pl.pallas_call(
        kernel,
        out_shape=shape_of((total, 4 * w), BF),
        in_specs=[SMEM] + [VMEM] * 4,
        out_specs=VMEM,
        scratch_shapes=[pltpu.VMEM((total, 4 * w), F32)],
        name="attn_weight_grads",
    )(me, x, d_qkv, d_proj, ctx)


def make_per_device(dp_count, tensor_count):
    def zx(array, step):
        return lax.ppermute(array, "tensor", [(i, i ^ step) for i in range(tensor_count)])

    def dx(array, step):
        return lax.ppermute(array, "dp", [(i, i ^ step) for i in range(dp_count)])

    def gather_group(piece):
        four = jnp.concatenate([piece] + [dx(piece, step) for step in (2, 4, 6)], axis=0)
        return four, dx(four, 1)

    def scatter_group(stacked):
        half = stacked.shape[0] // 2
        total = stacked[:half].astype(F32) + dx(stacked[half:], 1).astype(F32)
        quarter = half // 4
        out = total[:quarter]
        low = total[quarter:].astype(BF)
        for i, step in enumerate((2, 4, 6)):
            out = out + dx(low[i * quarter : (i + 1) * quarter], step).astype(F32)
        step = GROUP
        while step < dp_count:
            out = out + dx(out.astype(BF), step).astype(F32)
            step *= 2
        return out

    def per_device(
        tokens, lengths, dropped, queryproj, querybias, keyproj, valueproj, valuebias,
        outproj, outbias, gainone, shiftone, upproj, upbias, downproj, downbias,
        gaintwo, shifttwo, cotangent,
    ):
        share = cotangent.shape[0]
        width = tokens.shape[1]
        heads_width = queryproj.shape[1]
        z = lax.axis_index("tensor")
        me = lax.axis_index("dp") & (GROUP - 1)
        me_array = me.reshape(1)
        seq, half = z >> 1, z & 1
        length = lax.dynamic_index_in_dim(lengths, seq, 0, False)
        keep = 1.0 - lax.dynamic_index_in_dim(dropped, seq, 0, False).astype(F32)

        chunk = width // GROUP
        first = me * chunk
        piece_attn = jnp.concatenate(
            [lax.dynamic_slice_in_dim(a, first, chunk, 0) for a in (queryproj, keyproj, valueproj)]
            + [lax.dynamic_slice_in_dim(outproj, first, chunk, 1).T],
            axis=1,
        )
        piece_ffn = jnp.concatenate(
            [lax.dynamic_slice_in_dim(a, first, chunk, 0) for a in (upproj, downproj)], axis=0
        )
        biases = jnp.concatenate([querybias, valuebias, upbias]).reshape(1, -1)
        piece_attn = zx(piece_attn, 2)
        biases_far = zx(biases, 2)
        cot_far = zx(cotangent, 1)
        attn_halves = gather_group(piece_attn)
        piece_ffn = zx(piece_ffn, 2)
        ffn_halves = gather_group(piece_ffn)

        x_own = lax.dynamic_slice_in_dim(tokens, z * share, share, 0)
        x_far = lax.dynamic_slice_in_dim(tokens, (z ^ 1) * share, share, 0)
        x = jnp.concatenate([x_own, x_far], axis=0)
        base = jnp.arange(share, dtype=jnp.int32)
        position = jnp.concatenate([base + half * share, base + (1 - half) * share])
        valid = position < length
        bias_of = []
        for row in (biases[0], biases_far[0]):
            bias_of.append((row[:heads_width], row[heads_width : 2 * heads_width], row[2 * heads_width :]))

        pack_near = jnp.concatenate([queryproj, keyproj, valueproj, outproj.T], axis=1)
        packs = [pack_near]
        saved, partial = [], 0.0
        for block in range(2):
            if block == 1:
                packs.append(in_order(attn_halves, me_array, 1, BF)[0])
            keep_block, part = attn_forward(x, packs[block], *bias_of[block][:2], valid)
            saved.append(keep_block)
            partial = partial + part

        rows_of = (slice(0, share), slice(share, 2 * share))

        def pair_sum(parts):
            received = [zx(part.astype(BF), 1) for part in (parts[1], parts[0])]
            return [part + got.astype(F32) for part, got in zip(parts, received)]

        source = [x_own.astype(F32), x_far.astype(F32)]
        attention = pair_sum([partial[r] for r in rows_of])
        ups, downs = [upproj], [downproj]
        far_up, far_down = in_order(ffn_halves, me_array, 2, BF)
        ups.append(far_up)
        downs.append(far_down)
        first = [norm_forward(source[i] + attention[i] + outbias, gainone, shiftone) for i in range(2)]
        normed_low = [value[0].astype(BF) for value in first]
        acts, slopes, branches = [], [], []
        for i in range(2):
            branch = 0.0
            for block in range(2):
                act, slope = gelu_parts(nn(normed_low[i], ups[block]) + bias_of[block][2])
                acts.append(act.astype(BF))
                slopes.append(slope)
                branch = branch + nn(acts[-1], downs[block])
            branches.append(branch)
        branches = pair_sum(branches)
        cots = [cotangent, cot_far]
        d_outs, d_layers, d_mixeds, d_branches, d_inners, parts = [], [], [], [], [], []
        second = []
        for i in range(2):
            mixed = first[i][0] + branches[i] + downbias
            second.append(norm_forward(mixed, gaintwo, shifttwo))
            layer, normal_two, rscale_two = second[i]
            if i == 0:
                outputs = (keep * layer + (1.0 - keep) * source[0]).astype(BF)
            d_outs.append(cots[i].astype(F32) * valid[rows_of[i]].astype(F32)[:, None])
            d_layers.append(keep * d_outs[i])
            d_mixeds.append(norm_backward(d_layers[i], normal_two, rscale_two, gaintwo))
            d_branches.append(d_mixeds[i].astype(BF))
            part = 0.0
            for block in range(2):
                d_inner = nt(d_branches[i], downs[block]) * slopes[2 * i + block]
                d_inners.append(d_inner.astype(BF))
                part = part + nt(d_inners[-1], ups[block])
            parts.append(part)
        backs = pair_sum(parts)
        both = lambda pieces: jnp.concatenate(pieces, axis=0)
        up_sums, ffn_slices = [], []
        d_branch, normed_both = both(d_branches), both(normed_low)
        for block in range(2):
            d_inner, act = both(d_inners[block::2]), both(acts[block::2])
            up_sums.append(jnp.sum(d_inner, axis=0, dtype=F32))
            grads = weight_grads([(normed_both, d_inner), (act, d_branch)], me_array)
            ffn_slices.append(scatter_group(grads))
        d_normeds = [d_mixeds[i] + backs[i] for i in range(2)]
        d_attendeds = [norm_backward(d_normeds[i], *first[i][1:], gainone) for i in range(2)]
        d_proj = both([d.astype(BF) for d in d_attendeds])
        ffn_slice = ffn_slices[0] + zx(ffn_slices[1].astype(BF), 2).astype(F32)
        ffn_grads = in_order(gather_group(ffn_slice.astype(BF)), me_array, 2, F32)

        attn_slices, attn_sums, part = [], [], 0.0
        for block in (1, 0):
            grad, q_sum, v_sum, back = attn_backward(x, d_proj, packs[block], saved[block], valid, me_array)
            attn_slices.append(scatter_group(grad))
            attn_sums.append((q_sum, v_sum))
            part = part + back
        attn_slices.reverse()
        attn_sums.reverse()
        input_grad = (
            part[:share] + zx(part[share:].astype(BF), 1).astype(F32)
            + d_attendeds[0] + (1.0 - keep) * d_outs[0]
        )
        attn_slice = attn_slices[0] + zx(attn_slices[1].astype(BF), 2).astype(F32)
        grad_q, grad_k, grad_v, grad_o = attn_outputs(
            gather_group(attn_slice.astype(BF)), me_array, heads_width
        )

        rows = [
            jnp.sum(d_attendeds[0], axis=0),
            jnp.sum(d_normeds[0] * first[0][1], axis=0),
            jnp.sum(d_normeds[0], axis=0),
            jnp.sum(d_mixeds[0], axis=0),
            jnp.sum(d_layers[0] * second[0][1], axis=0),
            jnp.sum(d_layers[0], axis=0),
        ]
        pad = jnp.zeros((width - 2 * heads_width,), F32)
        near = jnp.stack(rows + [jnp.concatenate(attn_sums[0] + (pad,)), up_sums[0]])
        far = jnp.stack([jnp.concatenate(attn_sums[1] + (pad,)), up_sums[1]])
        small = jnp.concatenate([near, far], axis=0)
        step = 1
        while step < dp_count:
            small = small + dx(small, step)
            step *= 2
        vectors = small[:6]
        vectors = vectors + zx(vectors, 1)
        other = zx(jnp.concatenate([vectors, small[8:10]], axis=0), 2)
        vectors = vectors + other[:6]
        sums = small[6:8] + other[6:8]
        w = heads_width
        return (
            outputs,
            input_grad,
            grad_q,
            sums[0, :w],
            grad_k,
            grad_v,
            sums[0, w : 2 * w],
            grad_o,
            vectors[0],
            vectors[1],
            vectors[2],
            ffn_grads[0],
            sums[1],
            ffn_grads[1],
            vectors[3],
            vectors[4],
            vectors[5],
        )

    return per_device


def solution(mesh):
    both = P(("dp", "tensor"), None)
    column, row, unit = P(None, "tensor"), P("tensor", None), P("tensor")
    return jax.shard_map(
        make_per_device(mesh.shape["dp"], mesh.shape["tensor"]),
        mesh=mesh,
        in_specs=(
            P("dp", None), P("dp"), P("dp"), column, unit, column, column, unit, row,
            P(), P(), P(), column, unit, row, P(), P(), P(), both,
        ),
        out_specs=(
            both, both, column, unit, column, column, unit, row, P(), P(), P(),
            column, unit, row, P(), P(), P(),
        ),
        check_vma=False,
    )
```

```python
import jax
import jax.numpy as jnp
from jax import lax
from jax.experimental import pallas as pl
from jax.experimental.pallas import tpu as pltpu
from jax.sharding import PartitionSpec as P

HD = 64
L = 512
EPS = 1e-05
GROUP = 8
BF = jnp.bfloat16
F32 = jnp.float32


def nn(left, right):
    return jnp.dot(left, right, preferred_element_type=F32)


def nt(left, right):
    return lax.dot_general(left, right, (((1,), (1,)), ((), ())), preferred_element_type=F32)


def tn(left, right):
    return lax.dot_general(left, right, (((0,), (0,)), ((), ())), preferred_element_type=F32)


def gelu_parts(inner):
    cumul = 0.5 * (1.0 + jax.scipy.special.erf(inner * 0.7071067811865476))
    slope = cumul + inner * jnp.exp(-0.5 * inner * inner) * 0.3989422804014327
    return inner * cumul, slope


def norm_forward(value, gain, shift):
    center = jnp.mean(value, axis=-1, keepdims=True)
    centered = value - center
    rscale = lax.rsqrt(jnp.mean(centered * centered, axis=-1, keepdims=True) + EPS)
    normal = centered * rscale
    return normal * gain + shift, normal, rscale


def norm_backward(grad_rows, normal, rscale, gain):
    scaled = grad_rows * gain
    return rscale * (
        scaled
        - jnp.mean(scaled, axis=-1, keepdims=True)
        - normal * jnp.mean(scaled * normal, axis=-1, keepdims=True)
    )


RELATIVE = (0, 2, 4, 6, 1, 3, 5, 7)
SMEM = pl.BlockSpec(memory_space=pltpu.SMEM)
VMEM = pl.BlockSpec(memory_space=pltpu.VMEM)


def shape_of(shape, dtype):
    return jax.ShapeDtypeStruct(shape, dtype)


def chunk_at(me, rel, rows):
    return pl.ds(pl.multiple_of((me ^ rel) * rows, 32), rows)


def cost(flops, moved):
    return pl.CostEstimate(flops=flops, bytes_accessed=moved, transcendentals=0)


def in_order(pieces, me, count, dtype):
    rows, width = pieces[0].shape
    part = rows // count

    def kernel(me_ref, *refs):
        mine = me_ref[0]
        for rel, source in zip(RELATIVE, refs[:GROUP]):
            for i, out in enumerate(refs[GROUP:]):
                chunk = source[i * part : (i + 1) * part, :]
                out[chunk_at(mine, rel, part), :] = chunk.astype(dtype)

    size = GROUP * rows * width
    return pl.pallas_call(
        kernel,
        out_shape=[shape_of((GROUP * part, width), dtype)] * count,
        in_specs=[SMEM] + [VMEM] * GROUP,
        out_specs=[VMEM] * count,
        cost_estimate=cost(size, 6 * size),
        name="in_order",
    )(me, *pieces)


def attn_outputs(pieces, me, w):
    rows, width = pieces[0].shape

    def kernel(me_ref, *refs):
        mine = me_ref[0]
        scratch = refs[-1]
        for rel, source in zip(RELATIVE, refs[:GROUP]):
            scratch[chunk_at(mine, rel, rows), :] = source[...].astype(F32)
        for i, out in enumerate(refs[GROUP:-1]):
            out[...] = scratch[i * w : (i + 1) * w, :]

    return pl.pallas_call(
        kernel,
        out_shape=[shape_of((w, width), F32)] * 4,
        in_specs=[SMEM] + [VMEM] * GROUP,
        out_specs=[VMEM] * 4,
        scratch_shapes=[pltpu.VMEM((GROUP * rows, width), F32)],
        name="attn_outputs",
    )(me, *pieces)


def spread(scratch, mine, keep, send, index, count):
    rows = scratch.shape[0] // GROUP
    for j, rel in enumerate(RELATIVE):
        out = keep if j < GROUP // 2 else send
        start = ((j % (GROUP // 2)) * count + index) * rows
        out[start : start + rows, :] = scratch[chunk_at(mine, rel, rows), :].astype(BF)


def weight_grads(pairs, me):
    total, width = pairs[0][0][0].shape[1], pairs[0][1][0].shape[1]
    count = len(pairs)

    def kernel(me_ref, *refs):
        keep, send, scratch = refs[-3:]
        for i in range(count):
            a, b, c, d = refs[4 * i : 4 * i + 4]
            scratch[...] = tn(a[...], c[...]) + tn(b[...], d[...])
            spread(scratch, me_ref[0], keep, send, i, count)

    half = shape_of((total * count // 2, width), BF)
    return pl.pallas_call(
        kernel,
        out_shape=[half, half],
        in_specs=[SMEM] + [VMEM] * (4 * count),
        out_specs=[VMEM] * 2,
        scratch_shapes=[pltpu.VMEM((total, width), F32)],
        cost_estimate=cost(count * 4 * 256 * total * width, 8 << 20),
        name="weight_grads",
    )(me, *[array for left, right in pairs for array in left + right])


def softmax_of(q, k, key_ok):
    scores = jnp.where(key_ok, nt(q, k) * HD ** (-0.5), -1000000000.0)
    expon = jnp.exp(scores - jnp.max(scores, axis=-1, keepdims=True))
    return expon / jnp.sum(expon, axis=-1, keepdims=True)


def attn_forward(x, weights, qb, vb, key_ok, me):
    gathered = len(weights) > 1
    count = len(weights)
    rows, width = x.shape
    w = qb.shape[1]

    def kernel(me_ref, x_ref, qb_ref, vb_ref, ok_ref, *refs):
        qkv_ref, ctx_ref, near, far = refs[count : count + 4]
        pack = refs[0]
        if gathered:
            pack = refs[count + 4]
            part = width // GROUP
            for rel, source in zip(RELATIVE, refs[:GROUP]):
                pack[chunk_at(me_ref[0], rel, part), :] = source[...]
        ok = ok_ref[...] > 0.0
        bias = (qb_ref[...], 0.0, vb_ref[...])
        for i in range(3):
            made = nt(x_ref[...], pack[i * w : (i + 1) * w, :]) + bias[i]
            qkv_ref[:, i * w : (i + 1) * w] = made.astype(BF)
        for first in range(0, w, HD):
            q, k, v = (qkv_ref[:, i * w + first : i * w + first + HD] for i in range(3))
            prob = softmax_of(q, k, ok).astype(BF)
            ctx_ref[:, first : first + HD] = nn(prob, v).astype(BF)
        out = pack[3 * w :, :]
        near[...] = nn(ctx_ref[: rows // 2, :], out)
        far[...] = nn(ctx_ref[rows // 2 :, :], out)

    half = shape_of((rows // 2, width), F32)
    outs = [shape_of((rows, 3 * w), BF), shape_of((rows, w), BF), half, half]
    if gathered:
        outs.append(shape_of((4 * w, width), BF))
    return pl.pallas_call(
        kernel,
        out_shape=outs,
        in_specs=[SMEM] + [VMEM] * (4 + count),
        out_specs=[VMEM] * len(outs),
        cost_estimate=cost(2 << 30, 8 << 20),
        name="attn_forward",
    )(me, x, qb, vb, key_ok, *weights)


def attn_backward(x, d_projs, pack, qkv, ctx, key_ok, me):
    rows, width = x.shape
    w = ctx.shape[1]
    mid = rows // 2

    def kernel(me_ref, x_ref, p0, p1, pack_ref, qkv_ref, ctx_ref, ok_ref, keep, send, sums, near, far,
               scratch, d_qkv, d_ctx):
        ok = ok_ref[...] > 0.0
        out = pack_ref[3 * w :, :]
        d_ctx[:mid, :] = nt(p0[...], out).astype(BF)
        d_ctx[mid:, :] = nt(p1[...], out).astype(BF)
        scale = HD ** (-0.5)
        for first in range(0, w, HD):
            q, k, v = (qkv_ref[:, i * w + first : i * w + first + HD] for i in range(3))
            grad = d_ctx[:, first : first + HD]
            prob = softmax_of(q, k, ok)
            d_prob = nt(grad, v)
            centre = jnp.sum(prob * d_prob, axis=-1, keepdims=True)
            d_scores = (prob * (d_prob - centre)).astype(BF)
            made = (nn(d_scores, k) * scale, tn(d_scores, q) * scale, tn(prob.astype(BF), grad))
            for i in range(3):
                d_qkv[:, i * w + first : i * w + first + HD] = made[i].astype(BF)
        sums[...] = jnp.sum(d_qkv[...].astype(F32), axis=0, keepdims=True)
        near[...] = nn(d_qkv[:mid, :], pack_ref[: 3 * w, :])
        far[...] = nn(d_qkv[mid:, :], pack_ref[: 3 * w, :])
        scratch[: 3 * w, :] = tn(d_qkv[...], x_ref[...])
        scratch[3 * w :, :] = tn(ctx_ref[:mid, :], p0[...]) + tn(ctx_ref[mid:, :], p1[...])
        spread(scratch, me_ref[0], keep, send, 0, 1)

    part, half = shape_of((mid, width), F32), shape_of((2 * w, width), BF)
    return pl.pallas_call(
        kernel,
        out_shape=[half, half, shape_of((1, 3 * w), F32), part, part],
        in_specs=[SMEM] + [VMEM] * 7,
        out_specs=[VMEM] * 5,
        scratch_shapes=[
            pltpu.VMEM((4 * w, width), F32),
            pltpu.VMEM((rows, 3 * w), BF),
            pltpu.VMEM((rows, w), BF),
        ],
        cost_estimate=cost(5 << 30, 8 << 20),
        name="attn_backward",
    )(me, x, *d_projs, pack, qkv, ctx, key_ok)


def add_quarters(keep, got):
    quarter, width = keep.shape[0] // 4, keep.shape[1]

    def kernel(keep_ref, got_ref, *outs):
        for i, out in enumerate(outs):
            at = slice(i * quarter, (i + 1) * quarter)
            total = keep_ref[at, :].astype(F32) + got_ref[at, :].astype(F32)
            out[...] = total.astype(out.dtype)

    low = shape_of((quarter, width), BF)
    return pl.pallas_call(
        kernel,
        out_shape=[shape_of((quarter, width), F32), low, low, low],
        in_specs=[VMEM] * 2,
        out_specs=[VMEM] * 4,
        cost_estimate=cost(keep.size, 8 * keep.size),
        name="add_quarters",
    )(keep, got)


def make_per_device(dp_count, tensor_count):
    def zx(array, step):
        return lax.ppermute(array, "tensor", [(i, i ^ step) for i in range(tensor_count)])

    def dx(array, step):
        return lax.ppermute(array, "dp", [(i, i ^ step) for i in range(dp_count)])

    def gather_group(piece):
        pieces = [piece] + [dx(piece, step) for step in (2, 4, 6)]
        return pieces + [dx(got, 1) for got in pieces]

    def scatter_group(keep, send):
        out, *low = add_quarters(keep, dx(send, 1))
        for part, step in zip(low, (2, 4, 6)):
            out = out + dx(part, step).astype(F32)
        step = GROUP
        while step < dp_count:
            out = out + dx(out.astype(BF), step).astype(F32)
            step *= 2
        return out

    def per_device(
        tokens, lengths, dropped, queryproj, querybias, keyproj, valueproj, valuebias,
        outproj, outbias, gainone, shiftone, upproj, upbias, downproj, downbias,
        gaintwo, shifttwo, cotangent,
    ):
        share = cotangent.shape[0]
        width = tokens.shape[1]
        heads_width = queryproj.shape[1]
        z = lax.axis_index("tensor")
        me = lax.axis_index("dp") & (GROUP - 1)
        me_array = me.reshape(1)
        seq, half = z >> 1, z & 1
        length = lax.dynamic_index_in_dim(lengths, seq, 0, False)
        keep = 1.0 - lax.dynamic_index_in_dim(dropped, seq, 0, False).astype(F32)

        chunk = width // GROUP
        first = me * chunk
        pack_near = jnp.concatenate([queryproj.T, keyproj.T, valueproj.T, outproj], axis=0)
        piece_attn = lax.dynamic_slice_in_dim(pack_near, first, chunk, 0)
        piece_ffn = jnp.concatenate(
            [lax.dynamic_slice_in_dim(a, first, chunk, 0) for a in (upproj, downproj)], axis=0
        )
        biases = jnp.concatenate([querybias, valuebias, upbias]).reshape(1, -1)
        piece_attn = zx(piece_attn, 2)
        biases_far = zx(biases, 2)
        cot_far = zx(cotangent, 1)
        attn_pieces = gather_group(piece_attn)
        piece_ffn = zx(piece_ffn, 2)
        ffn_pieces = gather_group(piece_ffn)

        x_own = lax.dynamic_slice_in_dim(tokens, z * share, share, 0)
        x_far = lax.dynamic_slice_in_dim(tokens, (z ^ 1) * share, share, 0)
        x = jnp.concatenate([x_own, x_far], axis=0)
        base = jnp.arange(share, dtype=jnp.int32)
        position = jnp.concatenate([base + half * share, base + (1 - half) * share])
        valid = position < length
        bias_of = []
        for row in (biases, biases_far):
            bias_of.append(
                (row[:, :heads_width], row[:, heads_width : 2 * heads_width], row[:, 2 * heads_width :])
            )
        key_ok = valid.astype(F32)[None, :]
        qkv_near, ctx_near, *part_near = attn_forward(
            x, [pack_near], *bias_of[0][:2], key_ok, me_array
        )
        qkv_far, ctx_far, *part_far, pack_far = attn_forward(
            x, attn_pieces, *bias_of[1][:2], key_ok, me_array
        )
        partial = [near + far for near, far in zip(part_near, part_far)]
        rows_of = (slice(0, share), slice(share, 2 * share))

        def pair_sum(parts):
            received = [zx(part.astype(BF), 1) for part in (parts[1], parts[0])]
            return [part + got.astype(F32) for part, got in zip(parts, received)]

        source = [x_own.astype(F32), x_far.astype(F32)]
        attention = pair_sum(partial)
        ups, downs = [upproj], [downproj]
        far_up, far_down = in_order(ffn_pieces, me_array, 2, BF)
        ups.append(far_up)
        downs.append(far_down)
        first = [norm_forward(source[i] + attention[i] + outbias, gainone, shiftone) for i in range(2)]
        normed_low = [value[0].astype(BF) for value in first]
        acts, slopes, branches = [], [], []
        for i in range(2):
            branch = 0.0
            for block in range(2):
                act, slope = gelu_parts(nn(normed_low[i], ups[block]) + bias_of[block][2])
                acts.append(act.astype(BF))
                slopes.append(slope)
                branch = branch + nn(acts[-1], downs[block])
            branches.append(branch)
        branches = pair_sum(branches)
        cots = [cotangent, cot_far]
        d_outs, d_layers, d_mixeds, d_branches, d_inners, parts = [], [], [], [], [], []
        second = []
        for i in range(2):
            mixed = first[i][0] + branches[i] + downbias
            second.append(norm_forward(mixed, gaintwo, shifttwo))
            layer, normal_two, rscale_two = second[i]
            if i == 0:
                outputs = (keep * layer + (1.0 - keep) * source[0]).astype(BF)
            d_outs.append(cots[i].astype(F32) * valid[rows_of[i]].astype(F32)[:, None])
            d_layers.append(keep * d_outs[i])
            d_mixeds.append(norm_backward(d_layers[i], normal_two, rscale_two, gaintwo))
            d_branches.append(d_mixeds[i].astype(BF))
            part = 0.0
            for block in range(2):
                d_inner = nt(d_branches[i], downs[block]) * slopes[2 * i + block]
                d_inners.append(d_inner.astype(BF))
                part = part + nt(d_inners[-1], ups[block])
            parts.append(part)
        backs = pair_sum(parts)
        up_sums, ffn_slices = [None] * 2, [None] * 2
        for block in (1, 0):
            d_inner, act = d_inners[block::2], acts[block::2]
            up_sums[block] = sum(jnp.sum(d, axis=0, dtype=F32) for d in d_inner)
            grads = weight_grads([(normed_low, d_inner), (act, d_branches)], me_array)
            ffn_slices[block] = scatter_group(*grads)
        d_normeds = [d_mixeds[i] + backs[i] for i in range(2)]
        d_attendeds = [norm_backward(d_normeds[i], *first[i][1:], gainone) for i in range(2)]
        d_projs = [d.astype(BF) for d in d_attendeds]
        ffn_slice = ffn_slices[0] + zx(ffn_slices[1].astype(BF), 2).astype(F32)
        ffn_grads = in_order(gather_group(ffn_slice.astype(BF)), me_array, 2, F32)

        attn_slices, attn_sums, parts = [], [], []
        for pack, qkv, ctx in ((pack_far, qkv_far, ctx_far), (pack_near, qkv_near, ctx_near)):
            keep_half, send_half, sums, *back = attn_backward(
                x, d_projs, pack, qkv, ctx, key_ok, me_array
            )
            attn_slices.append(scatter_group(keep_half, send_half))
            attn_sums.append((sums[0, :heads_width], sums[0, 2 * heads_width :]))
            parts.append(back)
        attn_slices.reverse()
        attn_sums.reverse()
        part = [near + far for near, far in zip(*parts)]
        input_grad = (
            part[0] + zx(part[1].astype(BF), 1).astype(F32)
            + d_attendeds[0] + (1.0 - keep) * d_outs[0]
        )
        attn_slice = attn_slices[0] + zx(attn_slices[1].astype(BF), 2).astype(F32)
        grad_q, grad_k, grad_v, grad_o = attn_outputs(
            gather_group(attn_slice.astype(BF)), me_array, heads_width
        )

        rows = [
            jnp.sum(d_attendeds[0], axis=0),
            jnp.sum(d_normeds[0] * first[0][1], axis=0),
            jnp.sum(d_normeds[0], axis=0),
            jnp.sum(d_mixeds[0], axis=0),
            jnp.sum(d_layers[0] * second[0][1], axis=0),
            jnp.sum(d_layers[0], axis=0),
        ]
        pad = jnp.zeros((width - 2 * heads_width,), F32)
        near = jnp.stack(rows + [jnp.concatenate(attn_sums[0] + (pad,)), up_sums[0]])
        far = jnp.stack([jnp.concatenate(attn_sums[1] + (pad,)), up_sums[1]])
        small = jnp.concatenate([near, far], axis=0)
        step = 1
        while step < dp_count:
            small = small + dx(small, step)
            step *= 2
        vectors = small[:6]
        vectors = vectors + zx(vectors, 1)
        other = zx(jnp.concatenate([vectors, small[8:10]], axis=0), 2)
        vectors = vectors + other[:6]
        sums = small[6:8] + other[6:8]
        w = heads_width
        return (
            outputs,
            input_grad,
            grad_q.T,
            sums[0, :w],
            grad_k.T,
            grad_v.T,
            sums[0, w : 2 * w],
            grad_o,
            vectors[0],
            vectors[1],
            vectors[2],
            ffn_grads[0],
            sums[1],
            ffn_grads[1],
            vectors[3],
            vectors[4],
            vectors[5],
        )

    return per_device


def solution(mesh):
    both = P(("dp", "tensor"), None)
    column, row, unit = P(None, "tensor"), P("tensor", None), P("tensor")
    return jax.shard_map(
        make_per_device(mesh.shape["dp"], mesh.shape["tensor"]),
        mesh=mesh,
        in_specs=(
            P("dp", None), P("dp"), P("dp"), column, unit, column, column, unit, row,
            P(), P(), P(), column, unit, row, P(), P(), P(), both,
        ),
        out_specs=(
            both, both, column, unit, column, column, unit, row, P(), P(), P(),
            column, unit, row, P(), P(), P(),
        ),
        check_vma=False,
    )
```
